768 devices in a mesh: grp: 24 (over z, core), ep: 32 (over y, x).
Axes of the slice: x: 4, y: 8, z: 12, core: 2. Of those that a mesh axis runs over, the one named last changes fastest.
Arguments:
- tokens: bfloat16 [12288, 4096], P('grp', 'ep'), may hold values from -6 to 6
- grad_out: bfloat16 [12288, 4096], P('grp', 'ep'), may hold values from -1.5 to 1.5
- routes: int32 [12288, 2], P('grp'), may hold values from 0 to 11, as said below
- route_weights: float32 [12288, 2], P('grp'), may hold values from 0.1 to 1
- gate_weight: bfloat16 [24, 384, 4096], P('grp'), may hold values from -0.09375 to 0.09375
- up_weight: bfloat16 [24, 384, 4096], P('grp'), may hold values from -0.09375 to 0.09375
- down_weight: bfloat16 [24, 384, 4096], P('grp'), may hold values from -0.21875 to 0.21875
Outputs:
- grad_tokens: bfloat16 [12288, 4096], P('grp', 'ep')
- grad_gates: float32 [12288, 2], P('grp')
The draws below stay inside these ranges and needn't reach their ends.
Inputs may be any that keep to these rules, and one draw needn't show every extreme that they name: The 2 routes of a token name different experts. Among the routes of the 512 tokens of one group, no expert is named more than 128 times; in every draw one expert is named exactly 128 times in every group.
All inputs are finite; a program needn't handle non-finite values.
Results may differ from the reference program's by a relative error of at most 0.0065.
Values may be sent and summed in bfloat16 or wider, within the bound.
A program may use at most 64 MiB of HBM per device.

```python
import math
import jax
import jax.numpy as jnp
from jax import lax

D = 4096
FF = 768
TOP = 2
HALF = 384
EXPERTS = 12
TOKG = 512
TOKENS = 12288
CAP = 128
N_GRP = 24


def draw_routes(key, part):
    key_hot, key_groups = jax.random.split(key)
    hot_expert = jax.random.randint(key_hot, (), 0, EXPERTS).astype(jnp.int32)

    def one_group(group_key):
        sub_keys = jax.random.split(group_key, 5)
        others = jax.random.permutation(sub_keys[0], EXPERTS - 1).astype(jnp.int32) + 1
        ordering = (hot_expert + jnp.concatenate([jnp.zeros((1,), jnp.int32), others])) % EXPERTS
        offset_first = jax.random.randint(sub_keys[1], (), 0, EXPERTS - 1).astype(jnp.int32)
        offset_rest = jax.random.randint(sub_keys[2], (), 0, EXPERTS - 1).astype(jnp.int32)
        token_pos = jnp.arange(TOKG, dtype=jnp.int32)
        in_first = token_pos < CAP
        later_pos = 2 * (token_pos - CAP) + offset_rest
        lead_pos = jnp.where(in_first, 0, 1 + later_pos % (EXPERTS - 1))
        trail_pos = jnp.where(in_first, 1 + (token_pos + offset_first) % (EXPERTS - 1), 1 + (later_pos + 1) % (EXPERTS - 1))
        flipped = jax.random.randint(sub_keys[3], (TOKG,), 0, 2) == 1
        first_col = jnp.where(flipped, trail_pos, lead_pos)
        second_col = jnp.where(flipped, lead_pos, trail_pos)
        picked = ordering[jnp.stack([first_col, second_col], axis=1)]
        shuffle = jax.random.permutation(sub_keys[4], TOKG)
        return picked[shuffle]
    group_keys = jax.random.split(key_groups, TOKENS // TOKG)
    return jax.vmap(one_group)(group_keys).reshape(TOKENS, TOP).astype(jnp.int32)


def levels(key, extent, cuts, least, top_value):
    def one(dim, parts):
        draws = jax.random.uniform(jax.random.fold_in(jax.random.fold_in(key, 6), dim), (parts,), jnp.float32, least / len(cuts), top_value / len(cuts))
        return jnp.repeat(jnp.exp(draws), extent[dim] // parts).reshape((-1,) + (1,) * (len(extent) - dim - 1))

    loudness = one(*cuts[0])
    for cut in cuts[1:]:
        loudness = loudness * one(*cut)
    return loudness


def gaussian(own_key, shape, deviation, most, cuts=(), kind=jnp.bfloat16):
    factor_of = levels(own_key, shape, cuts, -0.22, 0.18) if cuts else 1.0
    result = jax.random.normal(own_key, shape, jnp.float32) * deviation * factor_of
    return jnp.minimum(jnp.maximum(result, -most), most).astype(kind)


def setup_inputs(seed: int = 0) -> dict:
    splits = jax.random.split(jax.random.key(seed), 8)
    return {
        "tokens": gaussian(splits[0], (TOKENS, D), 1.0, 6.0, ((0, 24), (1, 32))),
        "grad_out": gaussian(splits[1], (TOKENS, D), 0.25, 1.5, ((0, 24), (1, 32))),
        "routes": draw_routes(jax.random.fold_in(splits[7], 71), 0),
        "route_weights": jnp.clip(jnp.exp(math.log(1.0) - 2.3025851 * jax.random.uniform(splits[3], (TOKENS, TOP), jnp.float32) ** levels(splits[3], (TOKENS, TOP), ((0, 24),), -0.2, 0.2)), 0.1, 1.0),
        "gate_weight": gaussian(splits[4], (N_GRP, HALF, D), D ** -0.5, 0.09375, ((0, 24),)),
        "up_weight": gaussian(splits[5], (N_GRP, HALF, D), D ** -0.5, 0.09375, ((0, 24),)),
        "down_weight": gaussian(splits[6], (N_GRP, HALF, D), FF ** -0.5, 0.21875, ((0, 24),)),
    }


def half_terms(rows_in, rows_back, gate_half, up_half, down_half):
    contract = (((1,), (1,)), ((), ()))
    gate_pre = lax.dot_general(rows_in, gate_half, contract, preferred_element_type=jnp.float32)
    up_pre = lax.dot_general(rows_in, up_half, contract, preferred_element_type=jnp.float32)
    back_proj = lax.dot_general(rows_back, down_half, contract, preferred_element_type=jnp.float32)
    sigmoid_gate = jax.nn.sigmoid(gate_pre)
    active = gate_pre * sigmoid_gate
    hidden = (active * up_pre).astype(jnp.bfloat16)
    hidden = lax.optimization_barrier(hidden)
    inner_sum = jnp.sum(hidden.astype(jnp.float32) * back_proj, axis=1)
    grad_gate_pre = (back_proj * up_pre * sigmoid_gate * (1.0 + gate_pre * (1.0 - sigmoid_gate))).astype(jnp.bfloat16)
    grad_up_pre = (back_proj * active).astype(jnp.bfloat16)
    partial_value = jnp.dot(grad_gate_pre, gate_half, preferred_element_type=jnp.float32)
    partial_value = partial_value + jnp.dot(grad_up_pre, up_half, preferred_element_type=jnp.float32)
    return inner_sum, partial_value.astype(jnp.bfloat16)


def reference(tokens, grad_out, routes, route_weights, gate_weight, up_weight, down_weight):
    flat_expert = routes.reshape(-1).astype(jnp.int32)
    flat_token = (jnp.arange(TOKENS * TOP, dtype=jnp.int32) // TOP).astype(jnp.int32)
    flat_weight = route_weights.reshape(-1)
    row_limit = N_GRP * CAP

    def per_expert(state_pair, expert):
        grad_acc, gate_acc = state_pair
        chosen = jnp.argsort((flat_expert != expert).astype(jnp.int32), stable=True)[:row_limit].astype(jnp.int32)
        matched = flat_expert[chosen] == expert
        token_index = flat_token[chosen]
        rows_in = tokens[token_index]
        rows_back = grad_out[token_index]
        inner_first, part_first = half_terms(rows_in, rows_back, gate_weight[expert], up_weight[expert], down_weight[expert])
        other_half = expert + EXPERTS
        inner_second, part_second = half_terms(rows_in, rows_back, gate_weight[other_half], up_weight[other_half], down_weight[other_half])
        pair_sum = (part_first.astype(grad_acc.dtype) + part_second.astype(grad_acc.dtype)).astype(jnp.bfloat16)
        pair_sum = lax.optimization_barrier(pair_sum)
        route_scale = jnp.where(matched, flat_weight[chosen], jnp.zeros_like(flat_weight[chosen]))
        contrib = route_scale[:, None] * pair_sum.astype(grad_acc.dtype)
        grad_acc = grad_acc.at[token_index].add(contrib)
        gate_acc = gate_acc.at[chosen].add(jnp.where(matched, inner_first + inner_second, jnp.zeros_like(inner_first)))
        return (grad_acc, gate_acc), None

    start = (jnp.zeros((TOKENS, D), jnp.float32), jnp.zeros((TOKENS * TOP,), jnp.float32))
    (grad_acc, gate_acc), unused = lax.scan(per_expert, start, jnp.arange(EXPERTS, dtype=jnp.int32))
    return grad_acc.astype(jnp.bfloat16), gate_acc.reshape(TOKENS, TOP)
```

```python
import functools

import jax
import jax.numpy as jnp
from jax import lax
from jax.experimental import pallas as pl
from jax.experimental.pallas import tpu as pltpu
from jax.sharding import PartitionSpec as P

MESH = pl.DeviceIdType.MESH
LANES = 128
NT = (((1,), (1,)), ((), ()))


def kernel(
    dims,
    tok_ref,
    grad_ref,
    routes_ref,
    rw_ref,
    gate_hbm,
    up_hbm,
    down_hbm,
    out_ref,
    gates_ref,
    xb,
    gb,
    cb,
    sb,
    rl,
    rr,
    tl,
    tr,
    fin,
    wg,
    wu,
    wd,
    gate_s,
    up_s,
    inner_out,
    inner_in,
    a_send,
    a_recv,
    g_send,
    g_recv,
    s_send,
    s_recv,
    c_send,
    c_recv,
    r_send,
    r_recv,
    e_send,
    e_recv,
    w_sem,
):
    groups, ranks, rows, width, half = dims
    chips = groups // 2
    far = chips // 2
    experts = groups // 2
    grp = lax.axis_index("grp")
    rank = lax.axis_index("ep")
    z = grp // 2
    core = lax.rem(grp, 2)
    other = 1 - core
    right = lax.rem(z + 1, chips) * 2 + core
    left = lax.rem(z + chips - 1, chips) * 2 + core
    sibling = z * 2 + other
    ahead = (right, left)
    expert = lax.rem(grp, experts)
    mid = width // 2
    parts = (pl.ds(0, mid), pl.ds(mid, width + LANES - mid))

    weights = [
        pltpu.make_async_copy(src.at[0], dst, w_sem.at[i])
        for i, (src, dst) in enumerate(((gate_hbm, wg), (up_hbm, wu), (down_hbm, wd)))
    ]
    for copy in weights:
        copy.start()

    barrier = pltpu.get_barrier_semaphore()
    for peer in (right, left, sibling):
        pl.semaphore_signal(barrier, inc=1, device_id=(peer, rank), device_id_type=MESH)

    def greet(i, carry):
        pl.semaphore_signal(
            barrier, inc=1, device_id=(grp, lax.rem(rank + i, ranks)), device_id_type=MESH
        )
        return carry

    lax.fori_loop(1, ranks, greet, 0)

    token_lane = lax.broadcasted_iota(jnp.int32, (rows, rows * ranks), 1)
    token_row = lax.broadcasted_iota(jnp.int32, (rows, rows * ranks), 0)
    mine = token_lane == token_row + rank * rows
    lane = lax.broadcasted_iota(jnp.int32, (rows, LANES), 1)

    def column(values, k):
        return jnp.sum(jnp.where(mine, values[k : k + 1, :], 0.0), axis=1, keepdims=True)

    routes_f = routes_ref[...].astype(jnp.float32)
    rw_f = rw_ref[...]
    lane_f = lane.astype(jnp.float32)
    meta = jnp.zeros((rows, LANES), jnp.float32)
    for k in range(2):
        chosen = column(routes_f, k)
        weight = column(rw_f, k)
        high = weight.astype(jnp.bfloat16).astype(jnp.float32)
        low = weight - high
        meta = meta + jnp.where(lane_f == chosen, high, 0.0)
        meta = meta + jnp.where(lane_f == chosen + float(experts), low, 0.0)
    own_slot = (far, 1)
    xb[far, 1, core, :, pl.ds(width, LANES)] = meta.astype(jnp.bfloat16)
    own_rows = pl.ds(pl.multiple_of(rank * rows, rows), rows)
    own_cols = pl.ds(pl.multiple_of(rank * LANES, LANES), LANES)
    xb[far, 1, core, :, own_cols] = tok_ref[own_rows, :]
    gb[far, 1, core, :, own_cols] = grad_ref[own_rows, :]

    pl.semaphore_wait(barrier, 3 + ranks - 1)

    def enter(which, i):
        src, buf = ((tok_ref, xb), (grad_ref, gb))[which]
        peer = lax.rem(rank + i, ranks)
        return pltpu.make_async_remote_copy(
            src_ref=src.at[pl.ds(pl.multiple_of(peer * rows, rows), rows), :],
            dst_ref=buf.at[far, 1, core, :, own_cols],
            send_sem=a_send.at[which, i],
            recv_sem=a_recv.at[which, i],
            device_id=(grp, peer),
            device_id_type=MESH,
        )

    def landed(which, i):
        buf = (xb, gb)[which]
        peer = lax.rem(rank + ranks - i, ranks)
        here = buf.at[far, 1, core, :, pl.ds(pl.multiple_of(peer * LANES, LANES), LANES)]
        return pltpu.make_async_remote_copy(
            src_ref=here,
            dst_ref=here,
            send_sem=a_send.at[which, i],
            recv_sem=a_recv.at[which, i],
            device_id=(grp, peer),
            device_id_type=MESH,
        )

    for which in range(2):

        def send_in(i, carry):
            enter(which, i).start()
            return carry

        lax.fori_loop(1, ranks, send_in, 0)

    def ring(direction, which, step):
        buf = (xb, gb)[which]
        if isinstance(step, int) and step == 0:
            src = buf.at[far, 1, core]
        else:
            src = buf.at[step, direction, core]
        return pltpu.make_async_remote_copy(
            src_ref=src,
            dst_ref=buf.at[step + 1, direction if not (isinstance(step, int) and step == far - 1) else 0, core],
            send_sem=g_send.at[direction, which, step],
            recv_sem=g_recv.at[direction, which, step + 1],
            device_id=(ahead[direction], rank),
            device_id_type=MESH,
        )

    def ring_last(direction, which):
        buf = (xb, gb)[which]
        return pltpu.make_async_remote_copy(
            src_ref=buf.at[far - 1, direction, core],
            dst_ref=buf.at[far, 0, core],
            send_sem=g_send.at[direction, which, far - 1],
            recv_sem=g_recv.at[direction, which, far],
            device_id=(ahead[direction], rank),
            device_id_type=MESH,
        )

    def share(which, slot, side):
        buf = (xb, gb)[which]
        return pltpu.make_async_remote_copy(
            src_ref=buf.at[slot, side, core],
            dst_ref=buf.at[slot, side, core],
            send_sem=s_send.at[side, which, slot],
            recv_sem=s_recv.at[side, which, slot],
            device_id=(sibling, rank),
            device_id_type=MESH,
        )

    def shared(which, slot, side):
        buf = (xb, gb)[which]
        return pltpu.make_async_remote_copy(
            src_ref=buf.at[slot, side, other],
            dst_ref=buf.at[slot, side, other],
            send_sem=s_send.at[side, which, slot],
            recv_sem=s_recv.at[side, which, slot],
            device_id=(sibling, rank),
            device_id_type=MESH,
        )

    for which in range(2):

        def arrive(i, carry):
            landed(which, i).wait_recv()
            return carry

        lax.fori_loop(1, ranks, arrive, 0)
        for direction in range(2):
            ring(direction, which, 0).start()
        share(which, far, 1).start()

    for copy in weights:
        copy.wait()

    lanes_m = lax.broadcasted_iota(jnp.int32, (4 * rows, LANES), 1)

    def first_half(slot):
        for side in range(2):
            shared(0, slot, side).wait_recv()
        x = xb[slot, :, :, :, pl.ds(0, width)].reshape(4 * rows, width)
        gate_s[...] = lax.dot_general(x, wg[...], NT, preferred_element_type=jnp.float32)
        up_s[...] = lax.dot_general(x, wu[...], NT, preferred_element_type=jnp.float32)

    def hand_over(slot, side):
        return pltpu.make_async_remote_copy(
            src_ref=cb.at[slot, side, other],
            dst_ref=sb.at[slot, side],
            send_sem=c_send.at[side, slot],
            recv_sem=c_recv.at[side, slot],
            device_id=(sibling, rank),
            device_id_type=MESH,
        )

    def second_half(slot):
        for side in range(2):
            shared(1, slot, side).wait_recv()
        gr = gb[slot].reshape(4 * rows, width)
        back = lax.dot_general(gr, wd[...], NT, preferred_element_type=jnp.float32)
        gate_pre = gate_s[...]
        up_pre = up_s[...]
        sig = jax.nn.sigmoid(gate_pre)
        active = gate_pre * sig
        hidden = (active * up_pre).astype(jnp.bfloat16).astype(jnp.float32)
        inner = jnp.sum(hidden * back, axis=1, keepdims=True)
        d_gate = (back * up_pre * sig * (1.0 + gate_pre * (1.0 - sig))).astype(jnp.bfloat16)
        d_up = (back * active).astype(jnp.bfloat16)
        info = xb[slot, :, :, :, pl.ds(width, LANES)].reshape(4 * rows, LANES).astype(jnp.float32)
        picked = (lanes_m == expert) | (lanes_m == expert + experts)
        weight = jnp.sum(jnp.where(picked, info, 0.0), axis=1, keepdims=True)
        inner = jnp.where(weight > 0.0, inner, 0.0)
        high = inner.astype(jnp.bfloat16).astype(jnp.float32)
        low = inner - high
        extra = jnp.where(lanes_m == grp, high, jnp.where(lanes_m == grp + groups, low, 0.0))
        cb[slot, :, :, :, pl.ds(width, LANES)] = extra.astype(jnp.bfloat16).reshape(
            2, 2, rows, LANES
        )
        tile = 512

        def columns(n, carry):
            cols = pl.ds(pl.multiple_of(n * tile, tile), tile)
            part = jnp.dot(d_gate, wg[:, cols], preferred_element_type=jnp.float32)
            part = part + jnp.dot(d_up, wu[:, cols], preferred_element_type=jnp.float32)
            cb[slot, :, :, :, cols] = (weight * part).astype(jnp.bfloat16).reshape(
                2, 2, rows, tile
            )
            return carry

        lax.fori_loop(0, width // tile, columns, 0)
        for side in range(2):
            hand_over(slot, side).start()

    def step(t, carry):
        for which in range(2):

            @pl.when(t < far)
            def _():
                for direction in range(2):
                    ring(direction, which, t - 1).wait_recv()
                    share(which, t, direction).start()

            @pl.when(t < far - 1)
            def _():
                for direction in range(2):
                    ring(direction, which, t).start()

            @pl.when(t == far - 1)
            def _():
                ring_last(which, which).start()

            @pl.when(t == far)
            def _():
                ring_last(which, which).wait_recv()
                share(which, far, 0).start()

            @pl.when(t > 1)
            def _():
                (first_half, second_half)[which](t - 1)

        return carry

    lax.fori_loop(1, far + 2, step, 0)

    def returning(direction, part, distance):
        stage, land = ((tl, rl), (tr, rr))[direction]
        return pltpu.make_async_remote_copy(
            src_ref=stage.at[distance, :, parts[part]],
            dst_ref=land.at[distance - 1, :, parts[part]],
            send_sem=r_send.at[direction, part, distance],
            recv_sem=r_recv.at[direction, part, distance],
            device_id=((left, right)[direction], rank),
            device_id_type=MESH,
        )

    def own_terms(slot, side, cols):
        return cb[slot, side, core, :, cols].astype(jnp.float32) + sb[slot, side, :, cols].astype(
            jnp.float32
        )

    hand_over(far, 0).wait_recv()
    for direction in range(2):
        stage = (tl, tr)[direction]
        cols = parts[direction]
        stage[far, :, cols] = own_terms(far, 0, cols).astype(jnp.bfloat16)
        returning(direction, direction, far).start()
    for distance in range(far - 1, 0, -1):
        for direction in range(2):
            hand_over(distance, direction).wait_recv()
        for nth in range(2):
            for direction in range(2):
                stage, land = ((tl, rl), (tr, rr))[direction]
                part = nth if distance < far - 1 else (nth + 1 - direction) % 2
                cols = parts[part]
                value = own_terms(distance, direction, cols)
                if distance < far - 1 or part == direction:
                    returning(direction, part, distance + 1).wait_recv()
                    value = value + land[distance, :, cols].astype(jnp.float32)
                stage[distance, :, cols] = value.astype(jnp.bfloat16)
                returning(direction, part, distance).start()

    hand_over(far, 1).wait_recv()

    def leave(i):
        peer = lax.rem(rank + i, ranks)
        return pltpu.make_async_remote_copy(
            src_ref=fin.at[:, pl.ds(pl.multiple_of(peer * LANES, LANES), LANES)],
            dst_ref=out_ref.at[own_rows, :],
            send_sem=e_send.at[0, i],
            recv_sem=e_recv.at[0, i],
            device_id=(grp, peer),
            device_id_type=MESH,
        )

    def leave_inner(i):
        peer = lax.rem(rank + i, ranks)
        return pltpu.make_async_remote_copy(
            src_ref=inner_out,
            dst_ref=inner_in.at[rank],
            send_sem=e_send.at[1, i],
            recv_sem=e_recv.at[1, i],
            device_id=(grp, peer),
            device_id_type=MESH,
        )

    def back_home(i):
        peer = lax.rem(rank + ranks - i, ranks)
        here = out_ref.at[pl.ds(pl.multiple_of(peer * rows, rows), rows), :]
        return pltpu.make_async_remote_copy(
            src_ref=here,
            dst_ref=here,
            send_sem=e_send.at[0, i],
            recv_sem=e_recv.at[0, i],
            device_id=(grp, peer),
            device_id_type=MESH,
        )

    def back_home_inner(i):
        peer = lax.rem(rank + ranks - i, ranks)
        return pltpu.make_async_remote_copy(
            src_ref=inner_out,
            dst_ref=inner_in.at[peer],
            send_sem=e_send.at[1, i],
            recv_sem=e_recv.at[1, i],
            device_id=(grp, peer),
            device_id_type=MESH,
        )

    for part in range(2):
        cols = parts[part]
        for direction in range(2):
            returning(direction, part, 1).wait_recv()
        total = (
            own_terms(far, 1, cols)
            + rl[0, :, cols].astype(jnp.float32)
            + rr[0, :, cols].astype(jnp.float32)
        )
        if part == 0:
            fin[:, pl.ds(0, mid)] = total.astype(jnp.bfloat16)
        else:
            fin[:, pl.ds(mid, width - mid)] = total[:, : width - mid].astype(jnp.bfloat16)
            inner_lanes = total[:, width - mid :]

    place = (lane == lax.rem(rank, LANES // rows) * rows + lax.broadcasted_iota(
        jnp.int32, (rows, LANES), 0
    ))
    for k in range(2):
        chosen = column(routes_f, k)
        wanted = jnp.zeros((rows, LANES), jnp.bool_)
        for piece in range(4):
            wanted = wanted | (lane_f == chosen + float(piece * experts))
        gate_grad = jnp.sum(jnp.where(wanted, inner_lanes, 0.0), axis=1, keepdims=True)
        inner_out[k : k + 1, :] = jnp.sum(jnp.where(place, gate_grad, 0.0), axis=0, keepdims=True)

    def send_out(i, carry):
        leave(i).start()
        leave_inner(i).start()
        return carry

    lax.fori_loop(1, ranks, send_out, 0)
    out_ref[own_rows, :] = fin[:, own_cols]
    inner_in[rank] = inner_out[...]

    def drain_in(i, carry):
        for which in range(2):
            enter(which, i).wait_send()
        return carry

    lax.fori_loop(1, ranks, drain_in, 0)
    for which in range(2):
        for direction in range(2):
            ring(direction, which, 0).wait_send()
        share(which, far, 0).wait_send()
        share(which, far, 1).wait_send()
        ring_last(which, which).wait_send()
        for slot in range(1, far):
            for direction in range(2):
                share(which, slot, direction).wait_send()
                if slot < far - 1:
                    ring(direction, which, slot).wait_send()
    for slot in range(1, far + 1):
        for side in range(2):
            hand_over(slot, side).wait_send()
    for direction in range(2):
        returning(direction, direction, far).wait_send()
        for part in range(2):
            for distance in range(1, far):
                returning(direction, part, distance).wait_send()

    def finish(i, carry):
        back_home(i).wait_recv()
        back_home_inner(i).wait_recv()
        leave(i).wait_send()
        leave_inner(i).wait_send()
        return carry

    lax.fori_loop(1, ranks, finish, 0)
    per = LANES // rows
    for q in range(ranks // per):
        acc = inner_in[q * per]
        for j in range(1, per):
            acc = acc + inner_in[q * per + j]
        gates_ref[:, pl.ds(q * LANES, LANES)] = acc


def solution(mesh):
    groups, ranks = mesh.shape["grp"], mesh.shape["ep"]

    def on_device(tokens, grad_out, routes, route_weights, gate, up, down):
        count, feat = tokens.shape
        half, width = gate.shape[1:]
        rows = count // ranks
        far = groups // 4
        wide = width + LANES
        vmem = pl.BlockSpec(memory_space=pltpu.VMEM)
        hbm = pl.BlockSpec(memory_space=pl.ANY)
        dma = pltpu.SemaphoreType.DMA
        bf16, f32 = jnp.bfloat16, jnp.float32
        grad_tokens, grad_gates = pl.pallas_call(
            functools.partial(kernel, (groups, ranks, rows, width, half)),
            name="experts_backward",
            out_shape=(
                jax.ShapeDtypeStruct((count, feat), bf16),
                jax.ShapeDtypeStruct((2, count), f32),
            ),
            in_specs=[vmem, vmem, vmem, vmem, hbm, hbm, hbm],
            out_specs=(vmem, vmem),
            scratch_shapes=[
                pltpu.VMEM((far + 1, 2, 2, rows, wide), bf16),
                pltpu.VMEM((far + 1, 2, 2, rows, width), bf16),
                pltpu.VMEM((far + 1, 2, 2, rows, wide), bf16),
                pltpu.VMEM((far + 1, 2, rows, wide), bf16),
                pltpu.VMEM((far, rows, wide), bf16),
                pltpu.VMEM((far, rows, wide), bf16),
                pltpu.VMEM((far + 1, rows, wide), bf16),
                pltpu.VMEM((far + 1, rows, wide), bf16),
                pltpu.VMEM((rows, width), bf16),
                pltpu.VMEM((half, width), bf16),
                pltpu.VMEM((half, width), bf16),
                pltpu.VMEM((half, width), bf16),
                pltpu.VMEM((4 * rows, half), f32),
                pltpu.VMEM((4 * rows, half), f32),
                pltpu.VMEM((2, LANES), f32),
                pltpu.VMEM((ranks, 2, LANES), f32),
                dma((2, ranks)),
                dma((2, ranks)),
                dma((2, 2, far)),
                dma((2, 2, far + 1)),
                dma((2, 2, far + 1)),
                dma((2, 2, far + 1)),
                dma((2, far + 1)),
                dma((2, far + 1)),
                dma((2, 2, far + 1)),
                dma((2, 2, far + 1)),
                dma((2, ranks)),
                dma((2, ranks)),
                dma((3,)),
            ],
            compiler_params=pltpu.CompilerParams(
                collective_id=0, has_side_effects=True, vmem_limit_bytes=48 * 1024 * 1024
            ),
        )(tokens, grad_out, routes.T, route_weights.T, gate, up, down)
        return grad_tokens, grad_gates.T

    placed = (
        P("grp", "ep"),
        P("grp", "ep"),
        P("grp", None),
        P("grp", None),
        P("grp", None, None),
        P("grp", None, None),
        P("grp", None, None),
    )
    return jax.shard_map(
        on_device,
        mesh=mesh,
        in_specs=placed,
        out_specs=(P("grp", "ep"), P("grp", None)),
        check_vma=False,
    )
```

```python
import functools

import jax
import jax.numpy as jnp
from jax import lax
from jax.experimental import pallas as pl
from jax.experimental.pallas import tpu as pltpu
from jax.sharding import PartitionSpec as P

MESH = pl.DeviceIdType.MESH
LANES = 128
NT = (((1,), (1,)), ((), ()))


def kernel(
    dims,
    tok_hbm,
    grad_hbm,
    routes_hbm,
    rw_hbm,
    gate_hbm,
    up_hbm,
    down_hbm,
    out_ref,
    gates_ref,
    tok_ref,
    grad_ref,
    routes_ref,
    rw_ref,
    xb,
    gb,
    cb,
    sb,
    rl,
    rr,
    tl,
    tr,
    fin,
    wg,
    wu,
    wd,
    gate_s,
    up_s,
    inner_out,
    inner_in,
    a_send,
    a_recv,
    g_send,
    g_recv,
    s_send,
    s_recv,
    c_send,
    c_recv,
    r_send,
    r_recv,
    e_send,
    e_recv,
    w_sem,
    i_sem,
):
    groups, ranks, rows, width, half = dims
    chips = groups // 2
    far = chips // 2
    experts = groups // 2
    grp = lax.axis_index("grp")
    rank = lax.axis_index("ep")
    z = grp // 2
    core = lax.rem(grp, 2)
    other = 1 - core
    right = lax.rem(z + 1, chips) * 2 + core
    left = lax.rem(z + chips - 1, chips) * 2 + core
    sibling = z * 2 + other
    ahead = (right, left)
    expert = lax.rem(grp, experts)
    mid = width // 2
    parts = (pl.ds(0, LANES + mid), pl.ds(LANES + mid, width - mid))

    inputs = [
        pltpu.make_async_copy(src, dst, i_sem.at[i])
        for i, (src, dst) in enumerate(
            ((routes_hbm, routes_ref), (rw_hbm, rw_ref), (tok_hbm, tok_ref), (grad_hbm, grad_ref))
        )
    ]
    for copy in inputs:
        copy.start()
    weights = [
        pltpu.make_async_copy(src.at[0], dst, w_sem.at[i])
        for i, (src, dst) in enumerate(((gate_hbm, wg), (up_hbm, wu), (down_hbm, wd)))
    ]
    barrier = pltpu.get_barrier_semaphore()
    for peer in (right, left, sibling):
        pl.semaphore_signal(barrier, inc=1, device_id=(peer, rank), device_id_type=MESH)

    def greet(i, carry):
        pl.semaphore_signal(
            barrier, inc=1, device_id=(grp, lax.rem(rank + i, ranks)), device_id_type=MESH
        )
        return carry

    lax.fori_loop(1, ranks, greet, 0)
    for copy in weights:
        copy.start()
    for copy in inputs:
        copy.wait()

    token_lane = lax.broadcasted_iota(jnp.int32, (rows, rows * ranks), 1)
    token_row = lax.broadcasted_iota(jnp.int32, (rows, rows * ranks), 0)
    mine = token_lane == token_row + rank * rows
    lane = lax.broadcasted_iota(jnp.int32, (rows, LANES), 1)

    def column(values, k):
        return jnp.sum(jnp.where(mine, values[k : k + 1, :], 0.0), axis=1, keepdims=True)

    routes_f = routes_ref[...].astype(jnp.float32)
    rw_f = rw_ref[...]
    lane_f = lane.astype(jnp.float32)
    meta = jnp.zeros((rows, LANES), jnp.float32)
    for k in range(2):
        chosen = column(routes_f, k)
        weight = column(rw_f, k)
        high = weight.astype(jnp.bfloat16).astype(jnp.float32)
        low = weight - high
        meta = meta + jnp.where(lane_f == chosen, high, 0.0)
        meta = meta + jnp.where(lane_f == chosen + float(experts), low, 0.0)
    xb[far, 1, core, :, pl.ds(0, LANES)] = meta.astype(jnp.bfloat16)
    own_rows = pl.ds(pl.multiple_of(rank * rows, rows), rows)

    def features(which, owner):
        shift = LANES if which == 0 else 0
        return pl.ds(pl.multiple_of(owner * LANES + shift, LANES), LANES)

    xb[far, 1, core, :, features(0, rank)] = tok_ref[own_rows, :]
    gb[far, 1, core, :, features(1, rank)] = grad_ref[own_rows, :]

    pl.semaphore_wait(barrier, 3 + ranks - 1)

    def enter(which, i):
        src, buf = ((tok_ref, xb), (grad_ref, gb))[which]
        peer = lax.rem(rank + i, ranks)
        return pltpu.make_async_remote_copy(
            src_ref=src.at[pl.ds(pl.multiple_of(peer * rows, rows), rows), :],
            dst_ref=buf.at[far, 1, core, :, features(which, rank)],
            send_sem=a_send.at[which, i],
            recv_sem=a_recv.at[which, i],
            device_id=(grp, peer),
            device_id_type=MESH,
        )

    def landed(which, i):
        buf = (xb, gb)[which]
        peer = lax.rem(rank + ranks - i, ranks)
        here = buf.at[far, 1, core, :, features(which, peer)]
        return pltpu.make_async_remote_copy(
            src_ref=here,
            dst_ref=here,
            send_sem=a_send.at[which, i],
            recv_sem=a_recv.at[which, i],
            device_id=(grp, peer),
            device_id_type=MESH,
        )

    for which in range(2):

        def send_in(i, carry):
            enter(which, i).start()
            return carry

        lax.fori_loop(1, ranks, send_in, 0)

    def ring(direction, which, step):
        buf = (xb, gb)[which]
        if isinstance(step, int) and step == 0:
            src = buf.at[far, 1, core]
        else:
            src = buf.at[step, direction, core]
        return pltpu.make_async_remote_copy(
            src_ref=src,
            dst_ref=buf.at[step + 1, direction, core],
            send_sem=g_send.at[direction, which, step],
            recv_sem=g_recv.at[direction, which, step + 1],
            device_id=(ahead[direction], rank),
            device_id_type=MESH,
        )

    def ring_last(direction, which):
        buf = (xb, gb)[which]
        return pltpu.make_async_remote_copy(
            src_ref=buf.at[far - 1, direction, core],
            dst_ref=buf.at[far, 0, core],
            send_sem=g_send.at[direction, which, far - 1],
            recv_sem=g_recv.at[direction, which, far],
            device_id=(ahead[direction], rank),
            device_id_type=MESH,
        )

    def share(which, slot, side):
        buf = (xb, gb)[which]
        return pltpu.make_async_remote_copy(
            src_ref=buf.at[slot, side, core],
            dst_ref=buf.at[slot, side, core],
            send_sem=s_send.at[side, which, slot],
            recv_sem=s_recv.at[side, which, slot],
            device_id=(sibling, rank),
            device_id_type=MESH,
        )

    def shared(which, slot, side):
        buf = (xb, gb)[which]
        return pltpu.make_async_remote_copy(
            src_ref=buf.at[slot, side, other],
            dst_ref=buf.at[slot, side, other],
            send_sem=s_send.at[side, which, slot],
            recv_sem=s_recv.at[side, which, slot],
            device_id=(sibling, rank),
            device_id_type=MESH,
        )

    for which in range(2):

        def arrive(i, carry):
            landed(which, i).wait_recv()
            return carry

        lax.fori_loop(1, ranks, arrive, 0)
        for direction in range(2):
            ring(direction, which, 0).start()
        share(which, far, 1).start()

    for copy in weights:
        copy.wait()

    lanes_m = lax.broadcasted_iota(jnp.int32, (4 * rows, LANES), 1)

    def first_half(slot):
        for side in range(2):
            shared(0, slot, side).wait_recv()
        x = xb[slot, :, :, :, pl.ds(LANES, width)].reshape(4 * rows, width)
        gate_s[...] = lax.dot_general(x, wg[...], NT, preferred_element_type=jnp.float32)
        up_s[...] = lax.dot_general(x, wu[...], NT, preferred_element_type=jnp.float32)

    def hand_over(slot, side):
        return pltpu.make_async_remote_copy(
            src_ref=cb.at[slot, side, other],
            dst_ref=sb.at[slot, side],
            send_sem=c_send.at[side, slot],
            recv_sem=c_recv.at[side, slot],
            device_id=(sibling, rank),
            device_id_type=MESH,
        )

    def second_half(slot):
        for side in range(2):
            shared(1, slot, side).wait_recv()
        gr = gb[slot].reshape(4 * rows, width)
        back = lax.dot_general(gr, wd[...], NT, preferred_element_type=jnp.float32)
        gate_pre = gate_s[...]
        up_pre = up_s[...]
        sig = jax.nn.sigmoid(gate_pre)
        active = gate_pre * sig
        hidden = (active * up_pre).astype(jnp.bfloat16).astype(jnp.float32)
        inner = jnp.sum(hidden * back, axis=1, keepdims=True)
        d_gate = (back * up_pre * sig * (1.0 + gate_pre * (1.0 - sig))).astype(jnp.bfloat16)
        d_up = (back * active).astype(jnp.bfloat16)
        info = xb[slot, :, :, :, pl.ds(0, LANES)].reshape(4 * rows, LANES).astype(jnp.float32)
        picked = (lanes_m == expert) | (lanes_m == expert + experts)
        weight = jnp.sum(jnp.where(picked, info, 0.0), axis=1, keepdims=True)
        inner = jnp.where(weight > 0.0, inner, 0.0)
        high = inner.astype(jnp.bfloat16).astype(jnp.float32)
        low = inner - high
        extra = jnp.where(lanes_m == grp, high, jnp.where(lanes_m == grp + groups, low, 0.0))
        cb[slot, :, :, :, pl.ds(0, LANES)] = extra.astype(jnp.bfloat16).reshape(
            2, 2, rows, LANES
        )
        tile = 512

        def columns(n, carry):
            cols = pl.ds(pl.multiple_of(n * tile, tile), tile)
            part = jnp.dot(d_gate, wg[:, cols], preferred_element_type=jnp.float32)
            part = part + jnp.dot(d_up, wu[:, cols], preferred_element_type=jnp.float32)
            shifted = pl.ds(pl.multiple_of(n * tile + LANES, LANES), tile)
            cb[slot, :, :, :, shifted] = (weight * part).astype(jnp.bfloat16).reshape(
                2, 2, rows, tile
            )
            return carry

        lax.fori_loop(0, width // tile, columns, 0)
        for side in range(2):
            hand_over(slot, side).start()

    def pass_on(t, which):
        for direction in range(2):
            ring(direction, which, t - 1).wait_recv()

        @pl.when(t < far - 1)
        def _():
            for direction in range(2):
                ring(direction, which, t).start()

        @pl.when(t == far - 1)
        def _():
            ring_last(which, which).start()

        for direction in range(2):
            share(which, t, direction).start()

    def step(t, carry):
        @pl.when(t < far)
        def _():
            pass_on(t, 0)

        @pl.when(t > 1)
        def _():
            second_half(t - 1)

        @pl.when(t < far)
        def _():
            pass_on(t, 1)

        @pl.when(t == far)
        def _():
            for which in range(2):
                ring_last(which, which).wait_recv()
                share(which, far, 0).start()

        @pl.when(t < far + 1)
        def _():
            first_half(t)

        return carry

    lax.fori_loop(1, far + 2, step, 0)

    def returning(direction, part, distance):
        stage, land = ((tl, rl), (tr, rr))[direction]
        return pltpu.make_async_remote_copy(
            src_ref=stage.at[distance, :, parts[part]],
            dst_ref=land.at[distance - 1, :, parts[part]],
            send_sem=r_send.at[direction, part, distance],
            recv_sem=r_recv.at[direction, part, distance],
            device_id=((left, right)[direction], rank),
            device_id_type=MESH,
        )

    def own_terms(slot, side, cols):
        return cb[slot, side, core, :, cols].astype(jnp.float32) + sb[slot, side, :, cols].astype(
            jnp.float32
        )

    hand_over(far, 0).wait_recv()
    for direction in range(2):
        stage = (tl, tr)[direction]
        cols = parts[direction]
        stage[far, :, cols] = own_terms(far, 0, cols).astype(jnp.bfloat16)
        returning(direction, direction, far).start()
    for distance in range(far - 1, 0, -1):
        for direction in range(2):
            hand_over(distance, direction).wait_recv()
        for nth in range(2):
            for direction in range(2):
                stage, land = ((tl, rl), (tr, rr))[direction]
                part = nth if distance < far - 1 else (nth + 1 - direction) % 2
                cols = parts[part]
                value = own_terms(distance, direction, cols)
                if distance < far - 1 or part == direction:
                    returning(direction, part, distance + 1).wait_recv()
                    value = value + land[distance, :, cols].astype(jnp.float32)
                stage[distance, :, cols] = value.astype(jnp.bfloat16)
                returning(direction, part, distance).start()

    hand_over(far, 1).wait_recv()

    def leave(peer):
        return pltpu.make_async_remote_copy(
            src_ref=fin.at[:, features(0, peer)],
            dst_ref=out_ref.at[own_rows, :],
            send_sem=e_send.at[0, peer],
            recv_sem=e_recv.at[0, rank],
            device_id=(grp, peer),
            device_id_type=MESH,
        )

    def leave_inner(peer):
        return pltpu.make_async_remote_copy(
            src_ref=inner_out,
            dst_ref=inner_in.at[rank],
            send_sem=e_send.at[1, peer],
            recv_sem=e_recv.at[1, rank],
            device_id=(grp, peer),
            device_id_type=MESH,
        )

    def back_home(peer):
        here = out_ref.at[pl.ds(pl.multiple_of(peer * rows, rows), rows), :]
        return pltpu.make_async_remote_copy(
            src_ref=here,
            dst_ref=here,
            send_sem=e_send.at[0, peer],
            recv_sem=e_recv.at[0, peer],
            device_id=(grp, peer),
            device_id_type=MESH,
        )

    def back_home_inner(peer):
        return pltpu.make_async_remote_copy(
            src_ref=inner_out,
            dst_ref=inner_in.at[peer],
            send_sem=e_send.at[1, peer],
            recv_sem=e_recv.at[1, peer],
            device_id=(grp, peer),
            device_id_type=MESH,
        )

    place = lane == lax.rem(rank, LANES // rows) * rows + lax.broadcasted_iota(
        jnp.int32, (rows, LANES), 0
    )
    share_of = ranks // 2
    for part in range(2):
        cols = parts[part]
        for direction in range(2):
            returning(direction, part, 1).wait_recv()
        total = (
            own_terms(far, 1, cols)
            + rl[0, :, cols].astype(jnp.float32)
            + rr[0, :, cols].astype(jnp.float32)
        )
        fin[:, cols] = total.astype(jnp.bfloat16)

        def send_out(i, carry):
            peer = part * share_of + lax.rem(rank + i, share_of)

            @pl.when(peer != rank)
            def _():
                leave(peer).start()

            return carry

        lax.fori_loop(0, share_of, send_out, 0)
        if part == 0:
            inner_lanes = total[:, :LANES]
            for k in range(2):
                chosen = column(routes_f, k)
                wanted = jnp.zeros((rows, LANES), jnp.bool_)
                for piece in range(4):
                    wanted = wanted | (lane_f == chosen + float(piece * experts))
                gate_grad = jnp.sum(jnp.where(wanted, inner_lanes, 0.0), axis=1, keepdims=True)
                inner_out[k : k + 1, :] = jnp.sum(
                    jnp.where(place, gate_grad, 0.0), axis=0, keepdims=True
                )

            def send_inner(i, carry):
                leave_inner(lax.rem(rank + i, ranks)).start()
                return carry

            lax.fori_loop(1, ranks, send_inner, 0)

    stay = pltpu.make_async_copy(
        fin.at[:, features(0, rank)], out_ref.at[own_rows, :], i_sem.at[4]
    )
    stay.start()
    inner_in[rank] = inner_out[...]

    stay.wait()
    def drain_in(i, carry):
        for which in range(2):
            enter(which, i).wait_send()
        return carry

    lax.fori_loop(1, ranks, drain_in, 0)
    for which in range(2):
        for direction in range(2):
            ring(direction, which, 0).wait_send()
        share(which, far, 0).wait_send()
        share(which, far, 1).wait_send()
        ring_last(which, which).wait_send()
        for slot in range(1, far):
            for direction in range(2):
                share(which, slot, direction).wait_send()
                if slot < far - 1:
                    ring(direction, which, slot).wait_send()
    for slot in range(1, far + 1):
        for side in range(2):
            hand_over(slot, side).wait_send()
    for direction in range(2):
        returning(direction, direction, far).wait_send()
        for part in range(2):
            for distance in range(1, far):
                returning(direction, part, distance).wait_send()

    def finish(i, carry):
        peer = lax.rem(rank + i, ranks)
        back_home(peer).wait_recv()
        back_home_inner(peer).wait_recv()
        leave(peer).wait_send()
        leave_inner(peer).wait_send()
        return carry

    lax.fori_loop(1, ranks, finish, 0)
    per = LANES // rows
    for q in range(ranks // per):
        acc = inner_in[q * per]
        for j in range(1, per):
            acc = acc + inner_in[q * per + j]
        gates_ref[:, pl.ds(q * LANES, LANES)] = acc


def solution(mesh):
    groups, ranks = mesh.shape["grp"], mesh.shape["ep"]

    def on_device(tokens, grad_out, routes, route_weights, gate, up, down):
        count, feat = tokens.shape
        half, width = gate.shape[1:]
        rows = count // ranks
        far = groups // 4
        wide = width + LANES
        vmem = pl.BlockSpec(memory_space=pltpu.VMEM)
        hbm = pl.BlockSpec(memory_space=pltpu.HBM)
        dma = pltpu.SemaphoreType.DMA
        bf16, f32 = jnp.bfloat16, jnp.float32
        grad_tokens, grad_gates = pl.pallas_call(
            functools.partial(kernel, (groups, ranks, rows, width, half)),
            name="experts_backward",
            out_shape=(
                jax.ShapeDtypeStruct((count, feat), bf16),
                jax.ShapeDtypeStruct((2, count), f32),
            ),
            in_specs=[hbm] * 7,
            out_specs=(hbm, vmem),
            scratch_shapes=[
                pltpu.VMEM((count, feat), bf16),
                pltpu.VMEM((count, feat), bf16),
                pltpu.VMEM((2, count), jnp.int32),
                pltpu.VMEM((2, count), f32),
                pltpu.VMEM((far + 1, 2, 2, rows, wide), bf16),
                pltpu.VMEM((far + 1, 2, 2, rows, width), bf16),
                pltpu.VMEM((far + 1, 2, 2, rows, wide), bf16),
                pltpu.VMEM((far + 1, 2, rows, wide), bf16),
                pltpu.VMEM((far, rows, wide), bf16),
                pltpu.VMEM((far, rows, wide), bf16),
                pltpu.VMEM((far + 1, rows, wide), bf16),
                pltpu.VMEM((far + 1, rows, wide), bf16),
                pltpu.VMEM((rows, wide), bf16),
                pltpu.VMEM((half, width), bf16),
                pltpu.VMEM((half, width), bf16),
                pltpu.VMEM((half, width), bf16),
                pltpu.VMEM((4 * rows, half), f32),
                pltpu.VMEM((4 * rows, half), f32),
                pltpu.VMEM((2, LANES), f32),
                pltpu.VMEM((ranks, 2, LANES), f32),
                dma((2, ranks)),
                dma((2, ranks)),
                dma((2, 2, far)),
                dma((2, 2, far + 1)),
                dma((2, 2, far + 1)),
                dma((2, 2, far + 1)),
                dma((2, far + 1)),
                dma((2, far + 1)),
                dma((2, 2, far + 1)),
                dma((2, 2, far + 1)),
                dma((2, ranks)),
                dma((2, ranks)),
                dma((3,)),
                dma((5,)),
            ],
            compiler_params=pltpu.CompilerParams(
                collective_id=0, has_side_effects=True, vmem_limit_bytes=67043328
            ),
        )(tokens, grad_out, routes.T, route_weights.T, gate, up, down)
        return grad_tokens, grad_gates.T

    placed = (
        P("grp", "ep"),
        P("grp", "ep"),
        P("grp", None),
        P("grp", None),
        P("grp", None, None),
        P("grp", None, None),
        P("grp", None, None),
    )
    return jax.shard_map(
        on_device,
        mesh=mesh,
        in_specs=placed,
        out_specs=(P("grp", "ep"), P("grp", None)),
        check_vma=False,
    )
```

```python
import functools

import jax
import jax.numpy as jnp
from jax import lax
from jax.experimental import pallas as pl
from jax.experimental.pallas import tpu as pltpu
from jax.sharding import PartitionSpec as P

MESH = pl.DeviceIdType.MESH
LANES = 128
PARTS = 4
NT = (((1,), (1,)), ((), ()))


def kernel(
    dims,
    tok_hbm,
    grad_hbm,
    routes_hbm,
    rw_hbm,
    gate_hbm,
    up_hbm,
    down_hbm,
    out_ref,
    gates_ref,
    tok_ref,
    grad_ref,
    routes_ref,
    rw_ref,
    xb,
    gb,
    cb,
    sb,
    rl,
    rr,
    tl,
    tr,
    fin,
    wgu,
    wd,
    pre_s,
    inner_out,
    inner_in,
    a_send,
    a_recv,
    g_send,
    g_recv,
    s_send,
    s_recv,
    c_send,
    c_recv,
    r_send,
    r_recv,
    e_send,
    e_recv,
    w_sem,
    i_sem,
):
    groups, ranks, rows, width, half = dims
    chips = groups // 2
    far = chips // 2
    experts = groups // 2
    grp = lax.axis_index("grp")
    rank = lax.axis_index("ep")
    z = grp // 2
    core = lax.rem(grp, 2)
    other = 1 - core
    right = lax.rem(z + 1, chips) * 2 + core
    left = lax.rem(z + chips - 1, chips) * 2 + core
    sibling = z * 2 + other
    ahead = (right, left)
    expert = lax.rem(grp, experts)
    piece = width // PARTS
    parts = [pl.ds(0, LANES + piece)]
    parts += [pl.ds(LANES + p * piece, piece) for p in range(1, PARTS)]
    order = [
        [p for p in range(PARTS) if p % 2 != d] + [p for p in range(PARTS) if p % 2 == d]
        for d in range(2)
    ]

    inputs = [
        pltpu.make_async_copy(src, dst, i_sem.at[i])
        for i, (src, dst) in enumerate(
            ((routes_hbm, routes_ref), (rw_hbm, rw_ref), (tok_hbm, tok_ref), (grad_hbm, grad_ref))
        )
    ]
    for copy in inputs:
        copy.start()
    weights = [
        pltpu.make_async_copy(src.at[0], dst, w_sem.at[i])
        for i, (src, dst) in enumerate(
            (
                (gate_hbm, wgu.at[pl.ds(0, half), :]),
                (up_hbm, wgu.at[pl.ds(half, half), :]),
                (down_hbm, wd),
            )
        )
    ]
    barrier = pltpu.get_barrier_semaphore()
    for peer in (right, left, sibling):
        pl.semaphore_signal(barrier, inc=1, device_id=(peer, rank), device_id_type=MESH)

    def greet(i, carry):
        pl.semaphore_signal(
            barrier, inc=1, device_id=(grp, lax.rem(rank + i, ranks)), device_id_type=MESH
        )
        return carry

    lax.fori_loop(1, ranks, greet, 0)
    for copy in weights:
        copy.start()
    for copy in inputs:
        copy.wait()

    token_lane = lax.broadcasted_iota(jnp.int32, (rows, rows * ranks), 1)
    token_row = lax.broadcasted_iota(jnp.int32, (rows, rows * ranks), 0)
    mine = token_lane == token_row + rank * rows
    lane = lax.broadcasted_iota(jnp.int32, (rows, LANES), 1)

    def column(values, k):
        return jnp.sum(jnp.where(mine, values[k : k + 1, :], 0.0), axis=1, keepdims=True)

    routes_f = routes_ref[...].astype(jnp.float32)
    rw_f = rw_ref[...]
    lane_f = lane.astype(jnp.float32)
    meta = jnp.zeros((rows, LANES), jnp.float32)
    for k in range(2):
        chosen = column(routes_f, k)
        weight = column(rw_f, k)
        high = weight.astype(jnp.bfloat16).astype(jnp.float32)
        low = weight - high
        meta = meta + jnp.where(lane_f == chosen, high, 0.0)
        meta = meta + jnp.where(lane_f == chosen + float(experts), low, 0.0)
    xb[far, 1, core, :, pl.ds(0, LANES)] = meta.astype(jnp.bfloat16)
    own_rows = pl.ds(pl.multiple_of(rank * rows, rows), rows)

    def features(which, owner):
        shift = LANES if which == 0 else 0
        return pl.ds(pl.multiple_of(owner * LANES + shift, LANES), LANES)

    xb[far, 1, core, :, features(0, rank)] = tok_ref[own_rows, :]
    gb[far, 1, core, :, features(1, rank)] = grad_ref[own_rows, :]

    pl.semaphore_wait(barrier, 3 + ranks - 1)

    def enter(which, i):
        src, buf = ((tok_ref, xb), (grad_ref, gb))[which]
        peer = lax.rem(rank + i, ranks)
        return pltpu.make_async_remote_copy(
            src_ref=src.at[pl.ds(pl.multiple_of(peer * rows, rows), rows), :],
            dst_ref=buf.at[far, 1, core, :, features(which, rank)],
            send_sem=a_send.at[which, i],
            recv_sem=a_recv.at[which, i],
            device_id=(grp, peer),
            device_id_type=MESH,
        )

    def landed(which, i):
        buf = (xb, gb)[which]
        peer = lax.rem(rank + ranks - i, ranks)
        here = buf.at[far, 1, core, :, features(which, peer)]
        return pltpu.make_async_remote_copy(
            src_ref=here,
            dst_ref=here,
            send_sem=a_send.at[which, i],
            recv_sem=a_recv.at[which, i],
            device_id=(grp, peer),
            device_id_type=MESH,
        )

    for which in range(2):

        def send_in(i, carry):
            enter(which, i).start()
            return carry

        lax.fori_loop(1, ranks, send_in, 0)

    def ring(direction, which, step):
        buf = (xb, gb)[which]
        if isinstance(step, int) and step == 0:
            src = buf.at[far, 1, core]
        else:
            src = buf.at[step, direction, core]
        return pltpu.make_async_remote_copy(
            src_ref=src,
            dst_ref=buf.at[step + 1, direction, core],
            send_sem=g_send.at[direction, which, step],
            recv_sem=g_recv.at[direction, which, step + 1],
            device_id=(ahead[direction], rank),
            device_id_type=MESH,
        )

    def ring_last(direction, which):
        buf = (xb, gb)[which]
        return pltpu.make_async_remote_copy(
            src_ref=buf.at[far - 1, direction, core],
            dst_ref=buf.at[far, 0, core],
            send_sem=g_send.at[direction, which, far - 1],
            recv_sem=g_recv.at[direction, which, far],
            device_id=(ahead[direction], rank),
            device_id_type=MESH,
        )

    def share(which, slot, side):
        buf = (xb, gb)[which]
        return pltpu.make_async_remote_copy(
            src_ref=buf.at[slot, side, core],
            dst_ref=buf.at[slot, side, core],
            send_sem=s_send.at[side, which, slot],
            recv_sem=s_recv.at[side, which, slot],
            device_id=(sibling, rank),
            device_id_type=MESH,
        )

    def shared(which, slot, side):
        buf = (xb, gb)[which]
        return pltpu.make_async_remote_copy(
            src_ref=buf.at[slot, side, other],
            dst_ref=buf.at[slot, side, other],
            send_sem=s_send.at[side, which, slot],
            recv_sem=s_recv.at[side, which, slot],
            device_id=(sibling, rank),
            device_id_type=MESH,
        )

    for which in range(2):

        def arrive(i, carry):
            landed(which, i).wait_recv()
            return carry

        lax.fori_loop(1, ranks, arrive, 0)
        for direction in range(2):
            ring(direction, which, 0).start()
        share(which, far, 1).start()

    for copy in weights:
        copy.wait()

    lanes_m = lax.broadcasted_iota(jnp.int32, (4 * rows, LANES), 1)

    def first_half(slot):
        for side in range(2):
            shared(0, slot, side).wait_recv()
        x = xb[slot, :, :, :, pl.ds(LANES, width)].reshape(4 * rows, width)
        pre_s[...] = lax.dot_general(x, wgu[...], NT, preferred_element_type=jnp.float32)

    def hand_over(slot, side, part):
        return pltpu.make_async_remote_copy(
            src_ref=cb.at[slot, side, other, :, parts[part]],
            dst_ref=sb.at[slot, side, :, parts[part]],
            send_sem=c_send.at[side, part, slot],
            recv_sem=c_recv.at[side, part, slot],
            device_id=(sibling, rank),
            device_id_type=MESH,
        )

    def second_half(slot):
        for side in range(2):
            shared(1, slot, side).wait_recv()
        gr = gb[slot].reshape(4 * rows, width)
        back = lax.dot_general(gr, wd[...], NT, preferred_element_type=jnp.float32)
        gate_pre = pre_s[:, pl.ds(0, half)]
        up_pre = pre_s[:, pl.ds(half, half)]
        sig = jax.nn.sigmoid(gate_pre)
        active = gate_pre * sig
        hidden = (active * up_pre).astype(jnp.bfloat16).astype(jnp.float32)
        inner = jnp.sum(hidden * back, axis=1, keepdims=True)
        d_gate = (back * up_pre * sig * (1.0 + gate_pre * (1.0 - sig))).astype(jnp.bfloat16)
        d_up = (back * active).astype(jnp.bfloat16)
        info = xb[slot, :, :, :, pl.ds(0, LANES)].reshape(4 * rows, LANES).astype(jnp.float32)
        picked = (lanes_m == expert) | (lanes_m == expert + experts)
        weight = jnp.sum(jnp.where(picked, info, 0.0), axis=1, keepdims=True)
        inner = jnp.where(weight > 0.0, inner, 0.0)
        high = inner.astype(jnp.bfloat16).astype(jnp.float32)
        low = inner - high
        extra = jnp.where(lanes_m == grp, high, jnp.where(lanes_m == grp + groups, low, 0.0))
        cb[slot, :, :, :, pl.ds(0, LANES)] = extra.astype(jnp.bfloat16).reshape(
            2, 2, rows, LANES
        )
        d_both = jnp.concatenate([d_gate, d_up], axis=1)
        for p in range(PARTS):
            part = jnp.dot(
                d_both, wgu[:, pl.ds(p * piece, piece)], preferred_element_type=jnp.float32
            )
            cb[slot, :, :, :, pl.ds(LANES + p * piece, piece)] = (
                (weight * part).astype(jnp.bfloat16).reshape(2, 2, rows, piece)
            )
            for side in range(2):
                hand_over(slot, side, p).start()

    def pass_on(t, which):
        for direction in range(2):
            ring(direction, which, t - 1).wait_recv()

        @pl.when(t < far - 1)
        def _():
            for direction in range(2):
                ring(direction, which, t).start()

        @pl.when(t == far - 1)
        def _():
            ring_last(which, which).start()

        for direction in range(2):
            share(which, t, direction).start()

    def step(t, carry):
        @pl.when(t < far)
        def _():
            pass_on(t, 0)

        @pl.when(t > 1)
        def _():
            second_half(t - 1)

        @pl.when(t < far)
        def _():
            pass_on(t, 1)

        @pl.when(t == far)
        def _():
            for which in range(2):
                ring_last(which, which).wait_recv()
                share(which, far, 0).start()

        @pl.when(t < far + 1)
        def _():
            first_half(t)

        return carry

    lax.fori_loop(1, far + 2, step, 0)

    def returning(direction, part, distance):
        stage, land = ((tl, rl), (tr, rr))[direction]
        return pltpu.make_async_remote_copy(
            src_ref=stage.at[distance, :, parts[part]],
            dst_ref=land.at[distance - 1, :, parts[part]],
            send_sem=r_send.at[direction, part, distance],
            recv_sem=r_recv.at[direction, part, distance],
            device_id=((left, right)[direction], rank),
            device_id_type=MESH,
        )

    def own_terms(slot, side, cols):
        return cb[slot, side, core, :, cols].astype(jnp.float32) + sb[slot, side, :, cols].astype(
            jnp.float32
        )

    for part in range(PARTS):
        direction = part % 2
        stage = (tl, tr)[direction]
        cols = parts[part]
        hand_over(far, 0, part).wait_recv()
        stage[far, :, cols] = own_terms(far, 0, cols).astype(jnp.bfloat16)
        returning(direction, part, far).start()
    for distance in range(far - 1, 0, -1):
        for nth in range(PARTS):
            for direction in range(2):
                stage, land = ((tl, rl), (tr, rr))[direction]
                part = order[direction][nth]
                cols = parts[part]
                hand_over(distance, direction, part).wait_recv()
                value = own_terms(distance, direction, cols)
                if distance < far - 1 or part % 2 == direction:
                    returning(direction, part, distance + 1).wait_recv()
                    value = value + land[distance, :, cols].astype(jnp.float32)
                stage[distance, :, cols] = value.astype(jnp.bfloat16)
                returning(direction, part, distance).start()

    def leave(peer):
        return pltpu.make_async_remote_copy(
            src_ref=fin.at[:, features(0, peer)],
            dst_ref=out_ref.at[own_rows, :],
            send_sem=e_send.at[0, peer],
            recv_sem=e_recv.at[0, rank],
            device_id=(grp, peer),
            device_id_type=MESH,
        )

    def leave_inner(peer):
        return pltpu.make_async_remote_copy(
            src_ref=inner_out,
            dst_ref=inner_in.at[rank],
            send_sem=e_send.at[1, peer],
            recv_sem=e_recv.at[1, rank],
            device_id=(grp, peer),
            device_id_type=MESH,
        )

    def back_home(peer):
        here = out_ref.at[pl.ds(pl.multiple_of(peer * rows, rows), rows), :]
        return pltpu.make_async_remote_copy(
            src_ref=here,
            dst_ref=here,
            send_sem=e_send.at[0, peer],
            recv_sem=e_recv.at[0, peer],
            device_id=(grp, peer),
            device_id_type=MESH,
        )

    def back_home_inner(peer):
        return pltpu.make_async_remote_copy(
            src_ref=inner_out,
            dst_ref=inner_in.at[peer],
            send_sem=e_send.at[1, peer],
            recv_sem=e_recv.at[1, peer],
            device_id=(grp, peer),
            device_id_type=MESH,
        )

    place = lane == lax.rem(rank, LANES // rows) * rows + lax.broadcasted_iota(
        jnp.int32, (rows, LANES), 0
    )
    share_of = ranks // PARTS
    for part in range(PARTS):
        cols = parts[part]
        hand_over(far, 1, part).wait_recv()
        for direction in range(2):
            returning(direction, part, 1).wait_recv()
        total = (
            own_terms(far, 1, cols)
            + rl[0, :, cols].astype(jnp.float32)
            + rr[0, :, cols].astype(jnp.float32)
        )
        fin[:, cols] = total.astype(jnp.bfloat16)

        def send_out(i, carry):
            peer = part * share_of + lax.rem(rank + i, share_of)

            @pl.when(peer != rank)
            def _():
                leave(peer).start()

            return carry

        lax.fori_loop(0, share_of, send_out, 0)
        if part == 0:
            inner_lanes = total[:, :LANES]
            for k in range(2):
                chosen = column(routes_f, k)
                wanted = jnp.zeros((rows, LANES), jnp.bool_)
                for piece in range(4):
                    wanted = wanted | (lane_f == chosen + float(piece * experts))
                gate_grad = jnp.sum(jnp.where(wanted, inner_lanes, 0.0), axis=1, keepdims=True)
                inner_out[k : k + 1, :] = jnp.sum(
                    jnp.where(place, gate_grad, 0.0), axis=0, keepdims=True
                )

            def send_inner(i, carry):
                leave_inner(lax.rem(rank + i, ranks)).start()
                return carry

            lax.fori_loop(1, ranks, send_inner, 0)

    stay = pltpu.make_async_copy(
        fin.at[:, features(0, rank)], out_ref.at[own_rows, :], i_sem.at[4]
    )
    stay.start()
    inner_in[rank] = inner_out[...]

    stay.wait()
    def drain_in(i, carry):
        for which in range(2):
            enter(which, i).wait_send()
        return carry

    lax.fori_loop(1, ranks, drain_in, 0)
    for which in range(2):
        for direction in range(2):
            ring(direction, which, 0).wait_send()
        share(which, far, 0).wait_send()
        share(which, far, 1).wait_send()
        ring_last(which, which).wait_send()
        for slot in range(1, far):
            for direction in range(2):
                share(which, slot, direction).wait_send()
                if slot < far - 1:
                    ring(direction, which, slot).wait_send()
    for slot in range(1, far + 1):
        for side in range(2):
            for part in range(PARTS):
                hand_over(slot, side, part).wait_send()
    for direction in range(2):
        for part in range(PARTS):
            if part % 2 == direction:
                returning(direction, part, far).wait_send()
            for distance in range(1, far):
                returning(direction, part, distance).wait_send()

    def finish(i, carry):
        peer = lax.rem(rank + i, ranks)
        back_home(peer).wait_recv()
        back_home_inner(peer).wait_recv()
        leave(peer).wait_send()
        leave_inner(peer).wait_send()
        return carry

    lax.fori_loop(1, ranks, finish, 0)
    per = LANES // rows
    for q in range(ranks // per):
        acc = inner_in[q * per]
        for j in range(1, per):
            acc = acc + inner_in[q * per + j]
        gates_ref[:, pl.ds(q * LANES, LANES)] = acc


def solution(mesh):
    groups, ranks = mesh.shape["grp"], mesh.shape["ep"]

    def on_device(tokens, grad_out, routes, route_weights, gate, up, down):
        count, feat = tokens.shape
        half, width = gate.shape[1:]
        rows = count // ranks
        far = groups // 4
        wide = width + LANES
        vmem = pl.BlockSpec(memory_space=pltpu.VMEM)
        hbm = pl.BlockSpec(memory_space=pltpu.HBM)
        dma = pltpu.SemaphoreType.DMA
        bf16, f32 = jnp.bfloat16, jnp.float32
        grad_tokens, grad_gates = pl.pallas_call(
            functools.partial(kernel, (groups, ranks, rows, width, half)),
            name="experts_backward",
            out_shape=(
                jax.ShapeDtypeStruct((count, feat), bf16),
                jax.ShapeDtypeStruct((2, count), f32),
            ),
            in_specs=[hbm] * 7,
            out_specs=(hbm, vmem),
            scratch_shapes=[
                pltpu.VMEM((count, feat), bf16),
                pltpu.VMEM((count, feat), bf16),
                pltpu.VMEM((2, count), jnp.int32),
                pltpu.VMEM((2, count), f32),
                pltpu.VMEM((far + 1, 2, 2, rows, wide), bf16),
                pltpu.VMEM((far + 1, 2, 2, rows, width), bf16),
                pltpu.VMEM((far + 1, 2, 2, rows, wide), bf16),
                pltpu.VMEM((far + 1, 2, rows, wide), bf16),
                pltpu.VMEM((far, rows, wide), bf16),
                pltpu.VMEM((far, rows, wide), bf16),
                pltpu.VMEM((far + 1, rows, wide), bf16),
                pltpu.VMEM((far + 1, rows, wide), bf16),
                pltpu.VMEM((rows, wide), bf16),
                pltpu.VMEM((2 * half, width), bf16),
                pltpu.VMEM((half, width), bf16),
                pltpu.VMEM((4 * rows, 2 * half), f32),
                pltpu.VMEM((2, LANES), f32),
                pltpu.VMEM((ranks, 2, LANES), f32),
                dma((2, ranks)),
                dma((2, ranks)),
                dma((2, 2, far)),
                dma((2, 2, far + 1)),
                dma((2, 2, far + 1)),
                dma((2, 2, far + 1)),
                dma((2, PARTS, far + 1)),
                dma((2, PARTS, far + 1)),
                dma((2, PARTS, far + 1)),
                dma((2, PARTS, far + 1)),
                dma((2, ranks)),
                dma((2, ranks)),
                dma((3,)),
                dma((5,)),
            ],
            compiler_params=pltpu.CompilerParams(
                collective_id=0, has_side_effects=True, vmem_limit_bytes=67043328
            ),
        )(tokens, grad_out, routes.T, route_weights.T, gate, up, down)
        return grad_tokens, grad_gates.T

    placed = (
        P("grp", "ep"),
        P("grp", "ep"),
        P("grp", None),
        P("grp", None),
        P("grp", None, None),
        P("grp", None, None),
        P("grp", None, None),
    )
    return jax.shard_map(
        on_device,
        mesh=mesh,
        in_specs=placed,
        out_specs=(P("grp", "ep"), P("grp", None)),
        check_vma=False,
    )
```

```python
import functools

import jax
import jax.numpy as jnp
from jax import lax
from jax.experimental import pallas as pl
from jax.experimental.pallas import tpu as pltpu
from jax.sharding import PartitionSpec as P

MESH = pl.DeviceIdType.MESH
LANES = 128
PARTS = 4
NT = (((1,), (1,)), ((), ()))


def kernel(
    dims,
    tok_hbm,
    grad_hbm,
    routes_hbm,
    rw_hbm,
    gate_hbm,
    up_hbm,
    down_hbm,
    out_ref,
    gates_ref,
    tok_ref,
    grad_ref,
    routes_ref,
    rw_ref,
    xb,
    gb,
    cb,
    sb,
    rl,
    rr,
    tl,
    tr,
    fin,
    wgu,
    wd,
    pre_s,
    inner_out,
    inner_in,
    a_send,
    a_recv,
    g_send,
    g_recv,
    s_send,
    s_recv,
    c_send,
    c_recv,
    r_send,
    r_recv,
    e_send,
    e_recv,
    w_sem,
    i_sem,
):
    groups, ranks, rows, width, half = dims
    chips = groups // 2
    far = chips // 2
    experts = groups // 2
    grp = lax.axis_index("grp")
    rank = lax.axis_index("ep")
    z = grp // 2
    core = lax.rem(grp, 2)
    other = 1 - core
    right = lax.rem(z + 1, chips) * 2 + core
    left = lax.rem(z + chips - 1, chips) * 2 + core
    sibling = z * 2 + other
    ahead = (right, left)
    expert = lax.rem(grp, experts)
    piece = width // PARTS
    parts = [pl.ds(0, LANES + piece)]
    parts += [pl.ds(LANES + p * piece, piece) for p in range(1, PARTS)]
    order = [
        [p for p in range(PARTS) if p % 2 != d] + [p for p in range(PARTS) if p % 2 == d]
        for d in range(2)
    ]

    inputs = [
        pltpu.make_async_copy(src, dst, i_sem.at[i])
        for i, (src, dst) in enumerate(
            ((routes_hbm, routes_ref), (rw_hbm, rw_ref), (tok_hbm, tok_ref), (grad_hbm, grad_ref))
        )
    ]
    for copy in inputs:
        copy.start()
    weights = [
        pltpu.make_async_copy(src.at[0], dst, w_sem.at[i])
        for i, (src, dst) in enumerate(
            (
                (gate_hbm, wgu.at[pl.ds(0, half), :]),
                (up_hbm, wgu.at[pl.ds(half, half), :]),
                (down_hbm, wd),
            )
        )
    ]
    barrier = pltpu.get_barrier_semaphore()
    for peer in (right, left, sibling):
        pl.semaphore_signal(barrier, inc=1, device_id=(peer, rank), device_id_type=MESH)

    def greet(i, carry):
        pl.semaphore_signal(
            barrier, inc=1, device_id=(grp, lax.rem(rank + i, ranks)), device_id_type=MESH
        )
        return carry

    lax.fori_loop(1, ranks, greet, 0)
    for copy in weights:
        copy.start()
    for copy in inputs:
        copy.wait()

    token_lane = lax.broadcasted_iota(jnp.int32, (rows, rows * ranks), 1)
    token_row = lax.broadcasted_iota(jnp.int32, (rows, rows * ranks), 0)
    mine = token_lane == token_row + rank * rows
    lane = lax.broadcasted_iota(jnp.int32, (rows, LANES), 1)

    def column(values, k):
        return jnp.sum(jnp.where(mine, values[k : k + 1, :], 0.0), axis=1, keepdims=True)

    routes_f = routes_ref[...].astype(jnp.float32)
    rw_f = rw_ref[...]
    lane_f = lane.astype(jnp.float32)
    meta = jnp.zeros((rows, LANES), jnp.float32)
    for k in range(2):
        chosen = column(routes_f, k)
        weight = column(rw_f, k)
        high = weight.astype(jnp.bfloat16).astype(jnp.float32)
        low = weight - high
        meta = meta + jnp.where(lane_f == chosen, high, 0.0)
        meta = meta + jnp.where(lane_f == chosen + float(experts), low, 0.0)
    xb[far, 1, core, :, pl.ds(0, LANES)] = meta.astype(jnp.bfloat16)
    own_rows = pl.ds(pl.multiple_of(rank * rows, rows), rows)

    def features(which, owner):
        shift = LANES if which == 0 else 0
        return pl.ds(pl.multiple_of(owner * LANES + shift, LANES), LANES)

    xb[far, 1, core, :, features(0, rank)] = tok_ref[own_rows, :]
    gb[far, 1, core, :, features(1, rank)] = grad_ref[own_rows, :]

    pl.semaphore_wait(barrier, 3 + ranks - 1)

    def enter(which, i):
        src, buf = ((tok_ref, xb), (grad_ref, gb))[which]
        peer = lax.rem(rank + i, ranks)
        return pltpu.make_async_remote_copy(
            src_ref=src.at[pl.ds(pl.multiple_of(peer * rows, rows), rows), :],
            dst_ref=buf.at[far, 1, core, :, features(which, rank)],
            send_sem=a_send.at[which, i],
            recv_sem=a_recv.at[which, i],
            device_id=(grp, peer),
            device_id_type=MESH,
        )

    def landed(which, i):
        buf = (xb, gb)[which]
        peer = lax.rem(rank + ranks - i, ranks)
        here = buf.at[far, 1, core, :, features(which, peer)]
        return pltpu.make_async_remote_copy(
            src_ref=here,
            dst_ref=here,
            send_sem=a_send.at[which, i],
            recv_sem=a_recv.at[which, i],
            device_id=(grp, peer),
            device_id_type=MESH,
        )

    for which in range(2):

        def send_in(i, carry):
            enter(which, i).start()
            return carry

        lax.fori_loop(1, ranks, send_in, 0)

    def ring(direction, which, step):
        buf = (xb, gb)[which]
        if isinstance(step, int) and step == 0:
            src = buf.at[far, 1, core]
        else:
            src = buf.at[step, direction, core]
        return pltpu.make_async_remote_copy(
            src_ref=src,
            dst_ref=buf.at[step + 1, direction, core],
            send_sem=g_send.at[direction, which, step],
            recv_sem=g_recv.at[direction, which, step + 1],
            device_id=(ahead[direction], rank),
            device_id_type=MESH,
        )

    def ring_last(direction, which):
        buf = (xb, gb)[which]
        return pltpu.make_async_remote_copy(
            src_ref=buf.at[far - 1, direction, core],
            dst_ref=buf.at[far, 0, core],
            send_sem=g_send.at[direction, which, far - 1],
            recv_sem=g_recv.at[direction, which, far],
            device_id=(ahead[direction], rank),
            device_id_type=MESH,
        )

    def share(which, slot, side):
        buf = (xb, gb)[which]
        return pltpu.make_async_remote_copy(
            src_ref=buf.at[slot, side, core],
            dst_ref=buf.at[slot, side, core],
            send_sem=s_send.at[side, which, slot],
            recv_sem=s_recv.at[side, which, slot],
            device_id=(sibling, rank),
            device_id_type=MESH,
        )

    def shared(which, slot, side):
        buf = (xb, gb)[which]
        return pltpu.make_async_remote_copy(
            src_ref=buf.at[slot, side, other],
            dst_ref=buf.at[slot, side, other],
            send_sem=s_send.at[side, which, slot],
            recv_sem=s_recv.at[side, which, slot],
            device_id=(sibling, rank),
            device_id_type=MESH,
        )

    for which in range(2):

        def arrive(i, carry):
            landed(which, i).wait_recv()
            return carry

        lax.fori_loop(1, ranks, arrive, 0)
        for direction in range(2):
            ring(direction, which, 0).start()
        share(which, far, 1).start()

    for copy in weights:
        copy.wait()

    lanes_m = lax.broadcasted_iota(jnp.int32, (4 * rows, LANES), 1)

    def first_half(slot):
        for side in range(2):
            shared(0, slot, side).wait_recv()
        x = xb[slot, :, :, :, pl.ds(LANES, width)].reshape(4 * rows, width)
        pre_s[...] = lax.dot_general(x, wgu[...], NT, preferred_element_type=jnp.float32)

    def hand_over(slot, side, part):
        return pltpu.make_async_remote_copy(
            src_ref=cb.at[slot, side, other, :, parts[part]],
            dst_ref=sb.at[slot, side, :, parts[part]],
            send_sem=c_send.at[side, part, slot],
            recv_sem=c_recv.at[side, part, slot],
            device_id=(sibling, rank),
            device_id_type=MESH,
        )

    def second_half(slot):
        for side in range(2):
            shared(1, slot, side).wait_recv()
        gr = gb[slot].reshape(4 * rows, width)
        back = lax.dot_general(gr, wd[...], NT, preferred_element_type=jnp.float32)
        gate_pre = pre_s[:, pl.ds(0, half)]
        up_pre = pre_s[:, pl.ds(half, half)]
        sig = jax.nn.sigmoid(gate_pre)
        active = gate_pre * sig
        hidden = (active * up_pre).astype(jnp.bfloat16).astype(jnp.float32)
        inner = jnp.sum(hidden * back, axis=1, keepdims=True)
        d_gate = (back * up_pre * sig * (1.0 + gate_pre * (1.0 - sig))).astype(jnp.bfloat16)
        d_up = (back * active).astype(jnp.bfloat16)
        info = xb[slot, :, :, :, pl.ds(0, LANES)].reshape(4 * rows, LANES).astype(jnp.float32)
        picked = (lanes_m == expert) | (lanes_m == expert + experts)
        weight = jnp.sum(jnp.where(picked, info, 0.0), axis=1, keepdims=True)
        inner = jnp.where(weight > 0.0, inner, 0.0)
        high = inner.astype(jnp.bfloat16).astype(jnp.float32)
        low = inner - high
        extra = jnp.where(lanes_m == grp, high, jnp.where(lanes_m == grp + groups, low, 0.0))
        cb[slot, :, :, :, pl.ds(0, LANES)] = extra.astype(jnp.bfloat16).reshape(
            2, 2, rows, LANES
        )
        d_both = jnp.concatenate([d_gate, d_up], axis=1)
        for p in range(PARTS):
            part = jnp.dot(
                d_both, wgu[:, pl.ds(p * piece, piece)], preferred_element_type=jnp.float32
            )
            cb[slot, :, :, :, pl.ds(LANES + p * piece, piece)] = (
                (weight * part).astype(jnp.bfloat16).reshape(2, 2, rows, piece)
            )
            for side in range(2):
                hand_over(slot, side, p).start()

    def pass_on(t, which):
        for direction in range(2):
            ring(direction, which, t - 1).wait_recv()

        @pl.when(t < far - 1)
        def _():
            for direction in range(2):
                ring(direction, which, t).start()

        @pl.when(t == far - 1)
        def _():
            ring_last(which, which).start()

        for direction in range(2):
            share(which, t, direction).start()

    def step(t, carry):
        @pl.when(t < far)
        def _():
            pass_on(t, 0)

        @pl.when(t > 1)
        def _():
            second_half(t - 1)

        @pl.when(t < far)
        def _():
            pass_on(t, 1)

        @pl.when(t == far)
        def _():
            for which in range(2):
                ring_last(which, which).wait_recv()
                share(which, far, 0).start()

        @pl.when(t < far + 1)
        def _():
            first_half(t)

        return carry

    lax.fori_loop(1, far + 2, step, 0)

    def returning(direction, part, distance):
        stage, land = ((tl, rl), (tr, rr))[direction]
        return pltpu.make_async_remote_copy(
            src_ref=stage.at[distance, :, parts[part]],
            dst_ref=land.at[distance - 1, :, parts[part]],
            send_sem=r_send.at[direction, part, distance],
            recv_sem=r_recv.at[direction, part, distance],
            device_id=((left, right)[direction], rank),
            device_id_type=MESH,
        )

    def own_terms(slot, side, cols):
        return cb[slot, side, core, :, cols].astype(jnp.float32) + sb[slot, side, :, cols].astype(
            jnp.float32
        )

    for part in range(PARTS):
        direction = part % 2
        stage = (tl, tr)[direction]
        cols = parts[part]
        hand_over(far, 0, part).wait_recv()
        stage[far, :, cols] = own_terms(far, 0, cols).astype(jnp.bfloat16)
        returning(direction, part, far).start()
    for distance in range(far - 1, 0, -1):
        for nth in range(PARTS):
            for direction in range(2):
                stage, land = ((tl, rl), (tr, rr))[direction]
                part = order[direction][nth]
                cols = parts[part]
                hand_over(distance, direction, part).wait_recv()
                value = own_terms(distance, direction, cols)
                if distance < far - 1 or part % 2 == direction:
                    returning(direction, part, distance + 1).wait_recv()
                    value = value + land[distance, :, cols].astype(jnp.float32)
                stage[distance, :, cols] = value.astype(jnp.bfloat16)
                returning(direction, part, distance).start()

    def leave(peer):
        return pltpu.make_async_remote_copy(
            src_ref=fin.at[:, features(0, peer)],
            dst_ref=out_ref.at[own_rows, :],
            send_sem=e_send.at[0, peer],
            recv_sem=e_recv.at[0, rank],
            device_id=(grp, peer),
            device_id_type=MESH,
        )

    def leave_inner(peer):
        return pltpu.make_async_remote_copy(
            src_ref=inner_out,
            dst_ref=inner_in.at[rank],
            send_sem=e_send.at[1, peer],
            recv_sem=e_recv.at[1, rank],
            device_id=(grp, peer),
            device_id_type=MESH,
        )

    def back_home(peer):
        here = out_ref.at[pl.ds(pl.multiple_of(peer * rows, rows), rows), :]
        return pltpu.make_async_remote_copy(
            src_ref=here,
            dst_ref=here,
            send_sem=e_send.at[0, peer],
            recv_sem=e_recv.at[0, peer],
            device_id=(grp, peer),
            device_id_type=MESH,
        )

    def back_home_inner(peer):
        return pltpu.make_async_remote_copy(
            src_ref=inner_out,
            dst_ref=inner_in.at[peer],
            send_sem=e_send.at[1, peer],
            recv_sem=e_recv.at[1, peer],
            device_id=(grp, peer),
            device_id_type=MESH,
        )

    place = lane == lax.rem(rank, LANES // rows) * rows + lax.broadcasted_iota(
        jnp.int32, (rows, LANES), 0
    )
    share_of = ranks // PARTS
    for part in range(PARTS):
        cols = parts[part]
        hand_over(far, 1, part).wait_recv()
        for direction in range(2):
            returning(direction, part, 1).wait_recv()
        total = (
            own_terms(far, 1, cols)
            + rl[0, :, cols].astype(jnp.float32)
            + rr[0, :, cols].astype(jnp.float32)
        )
        fin[:, cols] = total.astype(jnp.bfloat16)

        def send_out(i, carry):
            peer = part * share_of + lax.rem(rank + i, share_of)

            @pl.when(peer != rank)
            def _():
                leave(peer).start()

            return carry

        lax.fori_loop(0, share_of, send_out, 0)
        if part == 0:
            inner_lanes = total[:, :LANES]
            for k in range(2):
                chosen = column(routes_f, k)
                wanted = jnp.zeros((rows, LANES), jnp.bool_)
                for piece in range(4):
                    wanted = wanted | (lane_f == chosen + float(piece * experts))
                gate_grad = jnp.sum(jnp.where(wanted, inner_lanes, 0.0), axis=1, keepdims=True)
                inner_out[k : k + 1, :] = jnp.sum(
                    jnp.where(place, gate_grad, 0.0), axis=0, keepdims=True
                )

            def send_inner(i, carry):
                leave_inner(lax.rem(rank + i, ranks)).start()
                return carry

            lax.fori_loop(1, ranks, send_inner, 0)

    stay = pltpu.make_async_copy(
        fin.at[:, features(0, rank)], out_ref.at[own_rows, :], i_sem.at[4]
    )
    stay.start()
    inner_in[rank] = inner_out[...]

    stay.wait()
    def drain_in(i, carry):
        for which in range(2):
            enter(which, i).wait_send()
        return carry

    lax.fori_loop(1, ranks, drain_in, 0)
    for which in range(2):
        for direction in range(2):
            ring(direction, which, 0).wait_send()
        share(which, far, 0).wait_send()
        share(which, far, 1).wait_send()
        ring_last(which, which).wait_send()
        for slot in range(1, far):
            for direction in range(2):
                share(which, slot, direction).wait_send()
                if slot < far - 1:
                    ring(direction, which, slot).wait_send()
    for slot in range(1, far + 1):
        for side in range(2):
            for part in range(PARTS):
                hand_over(slot, side, part).wait_send()
    for direction in range(2):
        for part in range(PARTS):
            if part % 2 == direction:
                returning(direction, part, far).wait_send()
            for distance in range(1, far):
                returning(direction, part, distance).wait_send()

    def finish(i, carry):
        peer = lax.rem(rank + i, ranks)
        back_home(peer).wait_recv()
        back_home_inner(peer).wait_recv()
        leave(peer).wait_send()
        leave_inner(peer).wait_send()
        return carry

    lax.fori_loop(1, ranks, finish, 0)
    per = LANES // rows
    for q in range(ranks // per):
        acc = inner_in[q * per]
        for j in range(1, per):
            acc = acc + inner_in[q * per + j]
        gates_ref[:, pl.ds(q * LANES, LANES)] = acc


def settle(rows_ref, gates_ref, rows_out, gates_out, rows_v, gates_v, sem):
    pairs = ((gates_ref, gates_v, gates_out), (rows_ref, rows_v, rows_out))
    reads = [pltpu.make_async_copy(a, b, sem.at[0, i]) for i, (a, b, c) in enumerate(pairs)]
    writes = [pltpu.make_async_copy(b, c, sem.at[1, i]) for i, (a, b, c) in enumerate(pairs)]
    for read in reads:
        read.start()
    for read, write in zip(reads, writes):
        read.wait()
        write.start()
    for write in writes:
        write.wait()


def solution(mesh):
    groups, ranks = mesh.shape["grp"], mesh.shape["ep"]

    def on_device(tokens, grad_out, routes, route_weights, gate, up, down):
        count, feat = tokens.shape
        half, width = gate.shape[1:]
        rows = count // ranks
        far = groups // 4
        wide = width + LANES
        vmem = pl.BlockSpec(memory_space=pltpu.VMEM)
        hbm = pl.BlockSpec(memory_space=pltpu.HBM)
        dma = pltpu.SemaphoreType.DMA
        bf16, f32 = jnp.bfloat16, jnp.float32
        grad_tokens, grad_gates = pl.pallas_call(
            functools.partial(kernel, (groups, ranks, rows, width, half)),
            name="experts_backward",
            out_shape=(
                jax.ShapeDtypeStruct((count, feat), bf16),
                jax.ShapeDtypeStruct((2, count), f32),
            ),
            in_specs=[hbm] * 7,
            out_specs=(hbm, vmem),
            scratch_shapes=[
                pltpu.VMEM((count, feat), bf16),
                pltpu.VMEM((count, feat), bf16),
                pltpu.VMEM((2, count), jnp.int32),
                pltpu.VMEM((2, count), f32),
                pltpu.VMEM((far + 1, 2, 2, rows, wide), bf16),
                pltpu.VMEM((far + 1, 2, 2, rows, width), bf16),
                pltpu.VMEM((far + 1, 2, 2, rows, wide), bf16),
                pltpu.VMEM((far + 1, 2, rows, wide), bf16),
                pltpu.VMEM((far, rows, wide), bf16),
                pltpu.VMEM((far, rows, wide), bf16),
                pltpu.VMEM((far + 1, rows, wide), bf16),
                pltpu.VMEM((far + 1, rows, wide), bf16),
                pltpu.VMEM((rows, wide), bf16),
                pltpu.VMEM((2 * half, width), bf16),
                pltpu.VMEM((half, width), bf16),
                pltpu.VMEM((4 * rows, 2 * half), f32),
                pltpu.VMEM((2, LANES), f32),
                pltpu.VMEM((ranks, 2, LANES), f32),
                dma((2, ranks)),
                dma((2, ranks)),
                dma((2, 2, far)),
                dma((2, 2, far + 1)),
                dma((2, 2, far + 1)),
                dma((2, 2, far + 1)),
                dma((2, PARTS, far + 1)),
                dma((2, PARTS, far + 1)),
                dma((2, PARTS, far + 1)),
                dma((2, PARTS, far + 1)),
                dma((2, ranks)),
                dma((2, ranks)),
                dma((3,)),
                dma((5,)),
            ],
            compiler_params=pltpu.CompilerParams(
                collective_id=0, has_side_effects=True, vmem_limit_bytes=67043328
            ),
        )(tokens, grad_out, routes.T, route_weights.T, gate, up, down)
        grad_tokens, grad_gates = pl.pallas_call(
            settle,
            name="settle",
            out_shape=(
                jax.ShapeDtypeStruct((count, feat), bf16),
                jax.ShapeDtypeStruct((2, count), f32),
            ),
            in_specs=[hbm, hbm],
            out_specs=(hbm, hbm),
            scratch_shapes=[
                pltpu.VMEM((count, feat), bf16),
                pltpu.VMEM((2, count), f32),
                dma((2, 2)),
            ],
            compiler_params=pltpu.CompilerParams(vmem_limit_bytes=67043328),
        )(grad_tokens, grad_gates)
        return grad_tokens, grad_gates.T

    placed = (
        P("grp", "ep"),
        P("grp", "ep"),
        P("grp", None),
        P("grp", None),
        P("grp", None, None),
        P("grp", None, None),
        P("grp", None, None),
    )
    return jax.shard_map(
        on_device,
        mesh=mesh,
        in_specs=placed,
        out_specs=(P("grp", "ep"), P("grp", None)),
        check_vma=False,
    )
```
